768 devices in a mesh: row: 24 (over z, core), col: 32 (over x, y).
Axes of the slice: x: 4, y: 8, z: 12, core: 2. Of those that a mesh axis runs over, the one named last changes fastest.
Arguments:
- blocks: bfloat16 [24, 32, 12, 128, 128], P('row', 'col'), may hold values from -1 to 1, as said below
- block_row: int32 [24, 32, 12], P('row', 'col'), may hold values from -1 to 383, as said below
- block_col: int32 [24, 32, 12], P('row', 'col'), may hold values from -1 to 383, as said below
Outputs:
- factor: bfloat16 [24, 32, 12, 128, 128], P('row', 'col')
- trace: float32 [], replicated
The draws below stay inside these ranges and needn't reach their ends.
Inputs may be any that keep to these rules, and one draw needn't show every extreme that they name: `block_row`: ids are -1 in exactly the empty slots. All filled blocks of one block row are held on one index of row, all filled blocks of one block column on one index of col. A slot is empty in block_col exactly where it is empty in block_row. `blocks`: X is symmetric: the block (j, i) is the transpose of the block (i, j). Empty slots hold arbitrary values.
All inputs are finite; a program needn't handle non-finite values.
Results may differ from the reference program's by a relative error of at most 0.001.
Values may be sent and summed in bfloat16 or wider, within the bound.
A program may use at most 128 MiB of HBM per device.

```python
import jax
import jax.numpy as jnp
from jax import lax

BS = 128
HALF = 10
CPG = 12
NB = 384
RPG = 16
PAIRS = 21
SLOTS = 12
N_ROW = 24
N_COL = 32


def layout(key):
    row_order = jax.random.permutation(jax.random.fold_in(key, 101), N_ROW)
    col_order = jax.random.permutation(jax.random.fold_in(key, 102), N_COL)
    row_residue = jnp.argsort(row_order).astype(jnp.int32)
    col_residue = jnp.argsort(col_order).astype(jnp.int32)
    row_ids = row_residue[:, None] + N_ROW * jnp.arange(RPG, dtype=jnp.int32)[None, :]
    col_ids = col_residue[:, None] + N_COL * jnp.arange(CPG, dtype=jnp.int32)[None, :]
    cand_rows = jnp.broadcast_to(row_ids[:, None, :, None], (N_ROW, N_COL, RPG, CPG)).reshape(N_ROW, N_COL, RPG * CPG)
    cand_cols = jnp.broadcast_to(col_ids[None, :, None, :], (N_ROW, N_COL, RPG, CPG)).reshape(N_ROW, N_COL, RPG * CPG)
    offset = (cand_rows - cand_cols) % NB
    distance = jnp.minimum(offset, NB - offset)
    filled = distance <= HALF
    keys = jax.random.split(jax.random.fold_in(key, 103), N_ROW * N_COL)
    orders = jax.vmap(lambda k: jax.random.permutation(k, RPG * CPG))(keys).reshape(N_ROW, N_COL, RPG * CPG)
    score = jnp.where(filled, 0, RPG * CPG) + orders
    picked = jnp.argsort(score, axis=-1)[..., :SLOTS]
    live = jnp.take_along_axis(filled, picked, axis=-1)
    rows = jnp.where(live, jnp.take_along_axis(cand_rows, picked, axis=-1), -1)
    cols = jnp.where(live, jnp.take_along_axis(cand_cols, picked, axis=-1), -1)
    return (rows.astype(jnp.int32), cols.astype(jnp.int32))


def draw_block_row(key, part):
    return layout(key)[0]


def draw_block_col(key, part):
    return layout(key)[1]


def draw_blocks(key, part):
    rows, cols = layout(key)
    scales = jnp.exp(jax.random.uniform(jax.random.fold_in(key, 104), (NB,), jnp.float32, -0.8, 0.8))
    live = rows >= 0
    serial = NB + jnp.arange(N_ROW * N_COL * SLOTS, dtype=jnp.int32).reshape(rows.shape)
    lower = jnp.where(live, jnp.minimum(rows, cols), serial)
    upper = jnp.where(live, jnp.maximum(rows, cols), 0)
    base = jax.random.fold_in(key, 105)

    def single(low_id, high_id):
        slot_key = jax.random.fold_in(jax.random.fold_in(base, low_id), high_id)
        return jax.random.normal(slot_key, (BS, BS), jnp.float32)
    raw = jax.vmap(single)(lower.reshape(-1), upper.reshape(-1)).reshape(N_ROW, N_COL, SLOTS, BS, BS)
    flipped = jnp.swapaxes(raw, -1, -2)
    mirrored = (raw + flipped) * 0.70710678
    shaped = jnp.where((rows < cols)[..., None, None], raw, jnp.where((rows > cols)[..., None, None], flipped, mirrored))
    row_scale = jnp.where(live, scales[jnp.maximum(rows, 0)], 1.0)
    col_scale = jnp.where(live, scales[jnp.maximum(cols, 0)], 1.0)
    factor = row_scale * col_scale / jnp.sqrt(jnp.float32(PAIRS * BS))
    scaled = jnp.clip(shaped * factor[..., None, None], -1.0, 1.0)
    return scaled.astype(jnp.bfloat16)


def setup_inputs(seed: int = 0) -> dict:
    arg_keys = jax.random.split(jax.random.key(seed), 4)
    blocks = draw_blocks(jax.random.fold_in(arg_keys[3], 71), 0)
    block_row = draw_block_row(jax.random.fold_in(arg_keys[3], 71), 0)
    block_col = draw_block_col(jax.random.fold_in(arg_keys[3], 71), 0)
    return {"blocks": blocks, "block_row": block_row, "block_col": block_col}


def pair_product(total, own_rows, own_cols, left, right, bound):
    left_blocks, left_rows, left_cols = left
    right_blocks, right_rows, right_cols = right
    left_count = left_rows.shape[0]
    right_count = right_rows.shape[0]
    match = (own_rows[:, None, None] >= 0) & (left_rows[None, :, None] == own_rows[:, None, None]) & (left_rows[None, :, None] >= 0)
    match = match & (left_cols[None, :, None] == right_rows[None, None, :]) & (right_rows[None, None, :] >= 0)
    match = match & (right_cols[None, None, :] == own_cols[:, None, None])
    chosen = jnp.sum(jnp.where(match, jnp.arange(right_count, dtype=jnp.int32), 0), axis=2).astype(jnp.int32)
    hit = jnp.any(match, axis=2)
    ranked = (jnp.cumsum(hit.astype(jnp.int32), axis=1) - 1).astype(jnp.int32)
    width = min(bound, left_count)
    places = jnp.arange(width, dtype=jnp.int32)
    select = hit[:, None, :] & (ranked[:, None, :] == places[None, :, None])
    left_index = jnp.sum(jnp.where(select, jnp.arange(left_count, dtype=jnp.int32)[None, None, :], 0), axis=2).astype(jnp.int32)
    right_index = jnp.sum(jnp.where(select, chosen[:, None, :], 0), axis=2).astype(jnp.int32)
    used = jnp.any(select, axis=2)
    left_pick = jnp.where(used[:, :, None, None], left_blocks[left_index], 0).astype(jnp.float32)
    right_pick = jnp.where(used[:, :, None, None], right_blocks[right_index], 0).astype(jnp.float32)
    return total + jnp.einsum('spxy,spyz->sxz', left_pick, right_pick)


def reference(blocks, block_row, block_col):
    def one_device(flat):
        grid_row = flat // N_COL
        grid_col = flat % N_COL
        own_rows = block_row[grid_row, grid_col]
        own_cols = block_col[grid_row, grid_col]
        left = (blocks[grid_row].reshape(N_COL * SLOTS, BS, BS), block_row[grid_row].reshape(N_COL * SLOTS), block_col[grid_row].reshape(N_COL * SLOTS))
        right = (blocks[:, grid_col].reshape(N_ROW * SLOTS, BS, BS), block_row[:, grid_col].reshape(N_ROW * SLOTS), block_col[:, grid_col].reshape(N_ROW * SLOTS))
        start = jnp.zeros((SLOTS, BS, BS), jnp.float32)
        square = pair_product(start, own_rows, own_cols, left, right, PAIRS)
        diagonal = ((own_rows == own_cols) & (own_rows >= 0)).astype(jnp.float32)
        identity = jnp.eye(BS, dtype=jnp.float32)
        factor = 1.5 * diagonal[:, None, None] * identity - 0.5 * square
        part = jnp.sum(diagonal * jnp.trace(square, axis1=1, axis2=2))
        return factor.astype(jnp.bfloat16), part

    factors, parts = lax.map(one_device, jnp.arange(N_ROW * N_COL, dtype=jnp.int32))
    return factors.reshape(N_ROW, N_COL, SLOTS, BS, BS), jnp.sum(parts) / (NB * BS)
```

```python
import functools
import heapq

import jax
import jax.numpy as jnp
from jax import lax
from jax.experimental import pallas as pl
from jax.experimental.pallas import tpu as pltpu
from jax.sharding import Mesh
from jax.sharding import PartitionSpec as P

HALF = 10
PAIRS = 2 * HALF + 1
QUERIES = 24
SLOTS = 12
BS = 128
NB = 384
AXES = ("z", "core", "x", "y")
NZ, NCORE, NX, NY = 12, 2, 4, 8
COL = ("x", "y")
ROW = ("z", "core")
MESH = pl.DeviceIdType.MESH

PART_A = 5
BODY = SLOTS * BS
LEFT_ROWS = BODY
SUMS = BODY
RIGHT_ROWS = BODY + 16
NOTHING = NB * NB
N_LEFT, N_RIGHT = NX * NY, NZ * NCORE
LEFT_ZERO = N_LEFT * LEFT_ROWS
RIGHT_ZERO = N_RIGHT * RIGHT_ROWS


def plan():
    size, need, rows = {}, {}, {}

    def add(name, link, first, last, after):
        size[name] = (link, (last - first) / BS)
        need[name] = after
        rows[name] = (first, last - first)

    cut = PART_A * BS
    add(("AX", "R", 1), "xR", 0, cut, [])
    add(("AX", "L", 1), "xL", 0, cut, [])
    add(("AX", "R", 2), "xR", 0, 2 * BS, [("AX", "R", 1)])
    add(("AX", "L", 2), "xL", 2 * BS, cut, [("AX", "L", 1)])
    came = {0: [], -1: [("AX", "R", 1)], 1: [("AX", "L", 1)], 2: [("AX", "R", 2), ("AX", "L", 2)]}
    for d in "UD":
        add(("BY", d, 1), "y" + d, cut, LEFT_ROWS, [])
        for h in (2, 3):
            add(("BY", d, h), "y" + d, cut, LEFT_ROWS, [("BY", d, h - 1)])
    add(("BY", "U", 4), "yU", cut, 8 * BS, [("BY", "U", 3)])
    add(("BY", "D", 4), "yD", 8 * BS, LEFT_ROWS, [("BY", "D", 3)])
    for dx in (0, -1, 1, 2):
        for d in "UD":
            add(("AY", d, 1, dx), "y" + d, 0, cut, came[dx])
            for h in (2, 3):
                add(("AY", d, h, dx), "y" + d, 0, cut, [("AY", d, h - 1, dx)])
        d = "U" if dx in (0, -1) else "D"
        add(("AY", d, 4, dx), "y" + d, 0, cut, [("AY", d, 3, dx)])
    came = {0: [], 4: [("BY", "U", 4), ("BY", "D", 4)]}
    for h in (1, 2, 3):
        came[-h], came[h] = [("BY", "U", h)], [("BY", "D", h)]
    for dy in (0, -1, 1, -2, 2, -3, 3, 4):
        for d in "RL":
            add(("BX", d, 1, dy), "x" + d, cut, LEFT_ROWS, came[dy])
        d = "R" if dy in (0, -1, 2, -3) else "L"
        add(("BX", d, 2, dy), "x" + d, cut, LEFT_ROWS, [("BX", d, 1, dy)])
    add(("CX", "R", 1), "xR", 0, 1, [])
    add(("CX", "L", 1), "xL", 0, 1, [])
    add(("CX", "R", 2), "xR", 0, 1, [("CX", "R", 1)])
    for d in "UD":
        for h in range(1, 5 if d == "U" else 4):
            after = [("CY", d, h - 1)] if h > 1 else [("CX", "R", 1), ("CX", "L", 1), ("CX", "R", 2)]
            add(("CY", d, h), "y" + d, 0, NX, after)
    add(("CS", "O", 0), "s", 0, 1, [])
    for d in "UD":
        for h in range(1, 7 if d == "U" else 6):
            add(("CZ", d, h), "z" + d, 0, NCORE, [("CZ", d, h - 1)] if h > 1 else [("CS", "O", 0)])
    half = BODY // 2
    for d in "UD":
        for h in range(1, 6):
            add(("ZZ", d, h), "z" + d, 0, RIGHT_ROWS, [("ZZ", d, h - 1)] if h > 1 else [])
    add(("ZZ", "U", 6), "zU", 0, half, [("ZZ", "U", 5)])
    add(("ZZ", "D", 6), "zD", half, RIGHT_ROWS, [("ZZ", "D", 5)])
    add(("SS", "O", 0), "s", 0, RIGHT_ROWS, [])
    for d in "UD":
        for h in range(1, 7):
            first, count = rows[("ZZ", d, h)]
            add(("SS", d, h), "s", first, first + count, [("ZZ", d, h)])
    return size, need, rows


def expected(size, need):
    rank = {"CX": -4, "CS": -3, "CY": -2, "CZ": -1, "AX": 0, "BY": 1, "AY": 2, "BX": 3, "ZZ": 4, "SS": 5}
    free, queue, order = {}, [], []
    pending = {m: set(after) for m, after in need.items()}

    def issue(m, now):
        link, blocks = size[m]
        free[link] = max(now, free.get(link, 0.0)) + blocks * (0.18 if link == "s" else 0.7)
        heapq.heappush(queue, (round(free[link] + 1.6, 6), len(order), list(size).index(m), m))

    first = sorted((m for m in size if not need[m]), key=lambda m: rank[m[0]])
    for m in first:
        issue(m, 0.0)
    while queue:
        now, _, _, m = heapq.heappop(queue)
        released = []
        for other, waits in pending.items():
            if m in waits:
                waits.discard(m)
                if not waits:
                    released.append(other)
        released.sort(key=lambda n: rank[n[0]])
        for other in released:
            issue(other, now)
        order.append((m, released))
    return first, order


SIZE, NEED, ROWS = plan()
FIRST, ORDER = expected(SIZE, NEED)
INDEX = {m: i for i, m in enumerate(SIZE)}
N_BULK = len(SIZE)
N_SEM = N_BULK + NX - 1 + NY - 1


def kernel(
    blocks, row_ids, col_ids, factor, trace, left, right, left_ids, right_ids, x_sums, y_sums, left_at, right_at,
    left_look, right_look, send, recv, local,
):
    z, core, x, y = (lax.axis_index(a) for a in AXES)

    def at(base, shift, extent):
        return lax.rem(base + (shift + extent), extent)

    def left_chunk(dx, dy):
        return (at(x, dx, NX) * NY + at(y, dy, NY)) * LEFT_ROWS

    def right_chunk(dz, which):
        return (at(z, dz, NZ) * NCORE + which) * RIGHT_ROWS

    def near(axis, shift):
        base, extent = {"x": (x, NX), "y": (y, NY), "z": (z, NZ)}[axis]
        return {axis: at(base, shift, extent)}

    own_left = left_chunk(0, 0)
    own_right = right_chunk(0, core)
    mine = [
        pltpu.make_async_copy(
            blocks, left.at[pl.ds(pl.multiple_of(own_left, 16), BODY), :], local.at[0]
        ),
        pltpu.make_async_copy(
            blocks, right.at[pl.ds(pl.multiple_of(own_right, 16), BODY), :], local.at[1]
        ),
    ]
    for copy in mine:
        copy.start()

    barrier = pltpu.get_barrier_semaphore()
    partners = [near(a, s) for a in ("x", "y", "z") for s in (1, -1)] + [{"core": 1 - core}]
    for partner in partners:
        pl.semaphore_signal(barrier, inc=1, device_id=partner, device_id_type=MESH)

    lane = lax.broadcasted_iota(jnp.int32, (1, BS), 1)
    code = jnp.full((1, BS), NOTHING, jnp.int32)
    for t in range(SLOTS):
        value = jnp.where(row_ids[t] >= 0, row_ids[t] * NB + col_ids[t], NOTHING)
        code = jnp.where(lane == t, value, code)
    left_ids[y * NX + x] = code
    right_ids[z * NCORE + core] = code
    left[pl.ds(LEFT_ZERO, BS), :] = jnp.zeros((BS, BS), jnp.bfloat16)
    right[pl.ds(RIGHT_ZERO, BS), :] = jnp.zeros((BS, BS), jnp.bfloat16)

    for copy in mine:
        copy.wait()

    total = jnp.zeros((8, BS), jnp.float32)
    for t in range(SLOTS):
        block = left[pl.ds(pl.multiple_of(own_left + t * BS, 16), BS), :].astype(jnp.float32)
        folded = jnp.sum((block * block).reshape(BS // 8, 8, BS), axis=0)
        total = total + jnp.where(row_ids[t] >= 0, folded, 0.0)
    part = jnp.sum(jnp.sum(total, axis=1, keepdims=True), axis=0, keepdims=True)
    high = part.astype(jnp.bfloat16).astype(jnp.float32)
    middle = (part - high).astype(jnp.bfloat16).astype(jnp.float32)
    low = part - high - middle
    row_iota = lax.broadcasted_iota(jnp.int32, (16, BS), 0)
    piece = jnp.where(row_iota == 0, high, jnp.where(row_iota == 1, middle, low))
    right[pl.ds(pl.multiple_of(own_right + SUMS, 16), 16), :] = jnp.where(
        row_iota < 3, piece, 0.0
    ).astype(jnp.bfloat16)

    pl.semaphore_wait(barrier, len(partners))

    def transfer(m):
        kind, d, h = m[:3]
        first, count = ROWS[m]
        sign = -1 if d in "RU" else 1
        step = sign * (h - 1)
        if kind in ("CX", "CY"):
            ref = left_ids
            where = y * NX + at(x, step, NX) if kind == "CX" else at(y, step, NY) * NX
            target = near(kind[1].lower(), -sign)
        elif kind in ("CS", "CZ"):
            ref = right_ids
            where = z * NCORE + core if kind == "CS" else at(z, step, NZ) * NCORE
            target = {"core": 1 - core} if kind == "CS" else near("z", -sign)
        elif kind in ("ZZ", "SS"):
            if kind == "SS":
                where = right_chunk(sign * h if h else 0, core)
                target = {"core": 1 - core}
            else:
                where = right_chunk(step, core)
                target = near("z", -sign)
            ref = right
        else:
            if kind == "AX":
                where = left_chunk(step, 0)
            elif kind == "BX":
                where = left_chunk(step, m[3])
            elif kind == "BY":
                where = left_chunk(0, step)
            else:
                where = left_chunk(m[3], step)
            target = near("x" if kind in ("AX", "BX") else "y", -sign)
            ref = left
        if kind[0] == "C":
            view = ref.at[pl.ds(where, count)]
        else:
            view = ref.at[pl.ds(pl.multiple_of(where + first, 16), count), :]
        i = INDEX[m]
        return pltpu.make_async_remote_copy(
            src_ref=view, dst_ref=view, send_sem=send.at[i], recv_sem=recv.at[i],
            device_id=target, device_id_type=MESH,
        )

    def sum_transfer(axis, k):
        ref, here = (x_sums, x) if axis == "x" else (y_sums, y)
        i = N_BULK + (k - 1 if axis == "x" else NX - 1 + k - 1)
        return pltpu.make_async_remote_copy(
            src_ref=ref.at[here], dst_ref=ref.at[here], send_sem=send.at[i], recv_sem=recv.at[i],
            device_id=near(axis, k), device_id_type=MESH,
        )

    query = lax.broadcasted_iota(jnp.int32, (QUERIES, BS), 0)
    spread = query == lax.broadcasted_iota(jnp.int32, (QUERIES, BS), 1)
    slot_of_lane = lax.broadcasted_iota(jnp.int32, (1, BS), 1) * (BS // 16)

    def look_up(ids, n, chunk_of, nothing, table, by_row):
        def one(s, carry):
            i, j = row_ids[s], col_ids[s]
            k = i - HALF + query
            k = jnp.where(k < 0, k + NB, jnp.where(k >= NB, k - NB, k))
            gap = jnp.abs(k - j)
            gap = jnp.minimum(gap, NB - gap)
            wanted = i * NB + k if by_row else k * NB + j
            wanted = jnp.where((query < PAIRS) & (gap <= HALF) & (i >= 0), wanted, -1)
            found = jnp.full((QUERIES, BS), -1, jnp.int32)
            for c in range(n):
                found = jnp.where(wanted == ids[c], slot_of_lane + chunk_of(c), found)
            found = jnp.max(found, axis=1, keepdims=True)
            found = jnp.where(found < 0, nothing, found)
            table[pl.ds(s, 1), :] = jnp.max(jnp.where(spread, found, 0), axis=0, keepdims=True)
            return carry

        lax.fori_loop(0, SLOTS, one, 0)

    for m in FIRST:
        transfer(m).start()
    last_right = max(i for i, (m, _) in enumerate(ORDER) if m[0] in ("ZZ", "SS"))
    for i, (m, released) in enumerate(ORDER):
        transfer(m).wait_recv()
        for other in released:
            transfer(other).start()
        if i == last_right:
            total = jnp.zeros((16, BS), jnp.float32)
            for c in range(N_RIGHT):
                total = total + right[pl.ds(c * RIGHT_ROWS + SUMS, 16), :].astype(jnp.float32)
            x_sums[x] = jnp.broadcast_to(jnp.sum(total, axis=0, keepdims=True), (8, BS))
            look_up(right_ids, N_RIGHT, lambda c: c * (RIGHT_ROWS // 16), RIGHT_ZERO // 16, right_at, False)
            for k in range(1, NX):
                sum_transfer("x", k).start()
        if i == min(last_right + 6, len(ORDER) - 1):
            for k in range(1, NX):
                sum_transfer("x", k).wait_recv()
            total = x_sums[0]
            for k in range(1, NX):
                total = total + x_sums[k]
            y_sums[y] = total
        if i == min(last_right + 8, len(ORDER) - 1):
            for k in range(1, NY):
                sum_transfer("y", k).start()
    look_up(
        left_ids, N_LEFT, lambda c: (c % NX * NY + c // NX) * (LEFT_ROWS // 16), LEFT_ZERO // 16, left_at, True
    )
    for k in range(1, NY):
        sum_transfer("y", k).wait_recv()
    total = y_sums[0]
    for k in range(1, NY):
        total = total + y_sums[k]
    trace[...] = total * (1.0 / (NB * BS))

    looks = [
        pltpu.make_async_copy(left_at, left_look, local.at[0]),
        pltpu.make_async_copy(right_at, right_look, local.at[1]),
    ]
    for copy in looks:
        copy.start()
    for copy in looks:
        copy.wait()

    eye = lax.broadcasted_iota(jnp.int32, (BS, BS), 0) == lax.broadcasted_iota(jnp.int32, (BS, BS), 1)

    def one_slot(s, carry):
        def fetch(ref, table, q):
            return ref[pl.ds(table[s, q] * 16, BS), :]

        square = jnp.zeros((BS, BS), jnp.float32)
        for q in range(0, PAIRS + 1, 2):
            a = jnp.concatenate([fetch(left, left_look, q), fetch(left, left_look, q + 1)], axis=1)
            b = jnp.concatenate([fetch(right, right_look, q), fetch(right, right_look, q + 1)], axis=0)
            square = square + jnp.dot(a, b, preferred_element_type=jnp.float32)
        scale = jnp.where((row_ids[s] == col_ids[s]) & (row_ids[s] >= 0), 1.5, 0.0)
        factor[s] = (jnp.where(eye, scale, 0.0) - 0.5 * square).astype(jnp.bfloat16)
        return carry

    lax.fori_loop(0, SLOTS, one_slot, 0)

    for m in SIZE:
        transfer(m).wait_send()
    for axis, extent in (("x", NX), ("y", NY)):
        for k in range(1, extent):
            sum_transfer(axis, k).wait_send()


def shards(blocks, block_row, block_col):
    smem = pl.BlockSpec(memory_space=pltpu.SMEM)
    vmem = pl.BlockSpec(memory_space=pltpu.VMEM)
    factor, trace = pl.pallas_call(
        kernel,
        out_shape=(
            jax.ShapeDtypeStruct((SLOTS, BS, BS), jnp.bfloat16),
            jax.ShapeDtypeStruct((8, BS), jnp.float32),
        ),
        in_specs=[pl.BlockSpec(memory_space=pl.ANY), smem, smem],
        out_specs=(vmem, vmem),
        scratch_shapes=[
            pltpu.VMEM((LEFT_ZERO + BS, BS), jnp.bfloat16),
            pltpu.VMEM((RIGHT_ZERO + BS, BS), jnp.bfloat16),
            pltpu.VMEM((N_LEFT, 1, BS), jnp.int32),
            pltpu.VMEM((N_RIGHT, 1, BS), jnp.int32),
            pltpu.VMEM((NX, 8, BS), jnp.float32),
            pltpu.VMEM((NY, 8, BS), jnp.float32),
            pltpu.VMEM((16, BS), jnp.int32),
            pltpu.VMEM((16, BS), jnp.int32),
            pltpu.SMEM((16, BS), jnp.int32),
            pltpu.SMEM((16, BS), jnp.int32),
            pltpu.SemaphoreType.DMA((N_SEM,)),
            pltpu.SemaphoreType.DMA((N_SEM,)),
            pltpu.SemaphoreType.DMA((2,)),
        ],
        compiler_params=pltpu.CompilerParams(collective_id=0, has_side_effects=True),
    )(blocks.reshape(BODY, BS), block_row.reshape(SLOTS), block_col.reshape(SLOTS))
    return factor[None, None], trace[0, 0]


def solution(mesh):
    torus = Mesh(mesh.devices.reshape(NZ, NCORE, NX, NY), AXES)
    return jax.shard_map(
        shards,
        mesh=torus,
        in_specs=(P(ROW, COL, None, None, None), P(ROW, COL, None), P(ROW, COL, None)),
        out_specs=(P(ROW, COL, None, None, None), P()),
        check_vma=False,
    )
```

```python
import functools
import heapq

import jax
import jax.numpy as jnp
from jax import lax
from jax.experimental import pallas as pl
from jax.experimental.pallas import tpu as pltpu
from jax.sharding import Mesh
from jax.sharding import PartitionSpec as P

HALF = 10
PAIRS = 2 * HALF + 1
QUERIES = 24
SLOTS = 12
BS = 128
NB = 384
AXES = ("z", "core", "x", "y")
NZ, NCORE, NX, NY = 12, 2, 4, 8
COL = ("x", "y")
ROW = ("z", "core")
MESH = pl.DeviceIdType.MESH

PART_A = (2, 3)
PART_B = (3, 4)
PART_Z = (6, 6)
BACKLOG = 4.0
BODY = SLOTS * BS
LEFT_ROWS = BODY
SUMS = BODY
RIGHT_ROWS = BODY + 16
NOTHING = NB * NB
N_LEFT, N_RIGHT = NX * NY, NZ * NCORE
LEFT_ZERO = N_LEFT * LEFT_ROWS
RIGHT_ZERO = N_RIGHT * RIGHT_ROWS


def plan():
    size, need, rows = {}, {}, {}

    def add(name, link, span, after):
        size[name] = (link, (span[1] - span[0]) / BS)
        need[name] = after
        rows[name] = (span[0], span[1] - span[0])

    def spans(parts, first):
        for count in parts:
            yield (first * BS, (first + count) * BS)
            first += count

    for p, span in enumerate(spans(PART_A, 0)):
        for d in "RL":
            add(("AX", d, 1, 0, p), "x" + d, span, [])
        d = "RL"[p % 2]
        add(("AX", d, 2, 0, p), "x" + d, span, [("AX", d, 1, 0, p)])
        came = {0: [], -1: [("AX", "R", 1, 0, p)], 1: [("AX", "L", 1, 0, p)], 2: [("AX", d, 2, 0, p)]}
        for dx in (0, -1, 1, 2):
            for d in "UD":
                add(("AY", d, 1, dx, p), "y" + d, span, came[dx])
                for h in (2, 3):
                    add(("AY", d, h, dx, p), "y" + d, span, [("AY", d, h - 1, dx, p)])
            d = "U" if (dx in (0, -1)) == (p % 2 == 0) else "D"
            add(("AY", d, 4, dx, p), "y" + d, span, [("AY", d, 3, dx, p)])
    for p, span in enumerate(spans(PART_B, sum(PART_A))):
        for d in "UD":
            add(("BY", d, 1, 0, p), "y" + d, span, [])
            for h in (2, 3):
                add(("BY", d, h, 0, p), "y" + d, span, [("BY", d, h - 1, 0, p)])
        d = "UD"[p % 2]
        add(("BY", d, 4, 0, p), "y" + d, span, [("BY", d, 3, 0, p)])
        came = {0: [], 4: [("BY", d, 4, 0, p)]}
        for h in (1, 2, 3):
            came[-h], came[h] = [("BY", "U", h, 0, p)], [("BY", "D", h, 0, p)]
        for dy in (0, -1, 1, -2, 2, -3, 3, 4):
            for d in "RL":
                add(("BX", d, 1, dy, p), "x" + d, span, came[dy])
            d = "R" if (dy in (0, -1, 2, -3)) == (p % 2 == 0) else "L"
            add(("BX", d, 2, dy, p), "x" + d, span, [("BX", d, 1, dy, p)])
    for p, span in enumerate(spans(PART_Z, 0)):
        if p == len(PART_Z) - 1:
            span = (span[0], RIGHT_ROWS)
        add(("SS", "O", 0, 0, p), "s", span, [])
        for d in "UD":
            for h in range(1, 7 if d == "UD"[p % 2] else 6):
                add(("ZZ", d, h, 0, p), "z" + d, span, [("ZZ", d, h - 1, 0, p)] if h > 1 else [])
                add(("SS", d, h, 0, p), "s", span, [("ZZ", d, h, 0, p)])
    add(("CX", "R", 1), "xR", (0, 1), [])
    add(("CX", "L", 1), "xL", (0, 1), [])
    add(("CX", "R", 2), "xR", (0, 1), [("CX", "R", 1)])
    for d in "UD":
        for h in range(1, 5 if d == "U" else 4):
            after = [("CY", d, h - 1)] if h > 1 else [("CX", "R", 1), ("CX", "L", 1), ("CX", "R", 2)]
            add(("CY", d, h), "y" + d, (0, NX), after)
    add(("CS", "O", 0), "s", (0, 1), [])
    for d in "UD":
        for h in range(1, 7 if d == "U" else 6):
            add(("CZ", d, h), "z" + d, (0, NCORE), [("CZ", d, h - 1)] if h > 1 else [("CS", "O", 0)])
    return size, need, rows


def expected(size, need):
    after = {m: [] for m in size}
    for m, waits in need.items():
        for other in waits:
            after[other].append(m)
    length = {}

    def duration(m):
        link, blocks = size[m]
        return blocks * (0.05 if link == "s" else 0.706)

    def chain(m):
        if m not in length:
            length[m] = 1.6 + duration(m) + max([chain(n) for n in after[m]], default=0.0)
        return length[m]

    number = {m: i for i, m in enumerate(size)}
    rank = {m: (m[0][0] != "C", -chain(m), number[m]) for m in size}
    pending = {m: set(waits) for m, waits in need.items()}
    free, queue, waiting = {}, [], {}

    def start(now):
        started = []
        for link in sorted(waiting):
            ready = sorted(waiting[link], key=lambda m: rank[m])
            while ready and (link == "s" or free.get(link, 0.0) - now < BACKLOG):
                m = ready.pop(0)
                free[link] = max(now, free.get(link, 0.0)) + duration(m)
                heapq.heappush(queue, (round(free[link] + 1.6, 6), len(started), number[m], m))
                started.append(m)
            waiting[link] = ready
        return started

    def release(m):
        waiting.setdefault(size[m][0], []).append(m)

    for m in size:
        if not need[m]:
            release(m)
    first, order, now = start(0.0), [], 0.0
    while queue:
        when, _, _, m = heapq.heappop(queue)
        now = max(now, when) + 0.05
        for other in after[m]:
            pending[other].discard(m)
            if not pending[other]:
                release(other)
        order.append((m, start(now), now))
    return first, order


SIZE, NEED, ROWS = plan()
FIRST, ORDER = expected(SIZE, NEED)
INDEX = {m: i for i, m in enumerate(SIZE)}
N_BULK = len(SIZE)
N_SEM = N_BULK + NX - 1 + NY - 1


def kernel(
    blocks, row_ids, col_ids, factor, trace, left, right, left_ids, right_ids, x_sums, y_sums, left_at, right_at,
    left_look, right_look, send, recv, local,
):
    z, core, x, y = (lax.axis_index(a) for a in AXES)

    def at(base, shift, extent):
        return lax.rem(base + (shift + extent), extent)

    def left_chunk(dx, dy):
        return (at(x, dx, NX) * NY + at(y, dy, NY)) * LEFT_ROWS

    def right_chunk(dz, which):
        return (at(z, dz, NZ) * NCORE + which) * RIGHT_ROWS

    def near(axis, shift):
        base, extent = {"x": (x, NX), "y": (y, NY), "z": (z, NZ)}[axis]
        return {axis: at(base, shift, extent)}

    own_left = left_chunk(0, 0)
    own_right = right_chunk(0, core)
    mine = [
        pltpu.make_async_copy(
            blocks, left.at[pl.ds(pl.multiple_of(own_left, 16), BODY), :], local.at[0]
        ),
        pltpu.make_async_copy(
            blocks, right.at[pl.ds(pl.multiple_of(own_right, 16), BODY), :], local.at[1]
        ),
    ]
    for copy in mine:
        copy.start()

    barrier = pltpu.get_barrier_semaphore()
    partners = [near(a, s) for a in ("x", "y", "z") for s in (1, -1)] + [{"core": 1 - core}]
    for partner in partners:
        pl.semaphore_signal(barrier, inc=1, device_id=partner, device_id_type=MESH)

    lane = lax.broadcasted_iota(jnp.int32, (1, BS), 1)
    code = jnp.full((1, BS), NOTHING, jnp.int32)
    for t in range(SLOTS):
        value = jnp.where(row_ids[t] >= 0, row_ids[t] * NB + col_ids[t], NOTHING)
        code = jnp.where(lane == t, value, code)
    left_ids[y * NX + x] = code
    right_ids[z * NCORE + core] = code
    left[pl.ds(LEFT_ZERO, BS), :] = jnp.zeros((BS, BS), jnp.bfloat16)
    right[pl.ds(RIGHT_ZERO, BS), :] = jnp.zeros((BS, BS), jnp.bfloat16)

    for copy in mine:
        copy.wait()

    total = jnp.zeros((8, BS), jnp.float32)
    for t in range(SLOTS):
        block = left[pl.ds(pl.multiple_of(own_left + t * BS, 16), BS), :].astype(jnp.float32)
        folded = jnp.sum((block * block).reshape(BS // 8, 8, BS), axis=0)
        total = total + jnp.where(row_ids[t] >= 0, folded, 0.0)
    part = jnp.sum(jnp.sum(total, axis=1, keepdims=True), axis=0, keepdims=True)
    high = part.astype(jnp.bfloat16).astype(jnp.float32)
    middle = (part - high).astype(jnp.bfloat16).astype(jnp.float32)
    low = part - high - middle
    row_iota = lax.broadcasted_iota(jnp.int32, (16, BS), 0)
    piece = jnp.where(row_iota == 0, high, jnp.where(row_iota == 1, middle, low))
    right[pl.ds(pl.multiple_of(own_right + SUMS, 16), 16), :] = jnp.where(
        row_iota < 3, piece, 0.0
    ).astype(jnp.bfloat16)

    pl.semaphore_wait(barrier, len(partners))

    def transfer(m):
        kind, d, h = m[:3]
        first, count = ROWS[m]
        sign = -1 if d in "RU" else 1
        step = sign * (h - 1)
        if kind in ("CX", "CY"):
            ref = left_ids
            where = y * NX + at(x, step, NX) if kind == "CX" else at(y, step, NY) * NX
            target = near(kind[1].lower(), -sign)
        elif kind in ("CS", "CZ"):
            ref = right_ids
            where = z * NCORE + core if kind == "CS" else at(z, step, NZ) * NCORE
            target = {"core": 1 - core} if kind == "CS" else near("z", -sign)
        elif kind in ("ZZ", "SS"):
            if kind == "SS":
                where = right_chunk(sign * h if h else 0, core)
                target = {"core": 1 - core}
            else:
                where = right_chunk(step, core)
                target = near("z", -sign)
            ref = right
        else:
            if kind == "AX":
                where = left_chunk(step, 0)
            elif kind == "BX":
                where = left_chunk(step, m[3])
            elif kind == "BY":
                where = left_chunk(0, step)
            else:
                where = left_chunk(m[3], step)
            target = near("x" if kind in ("AX", "BX") else "y", -sign)
            ref = left
        if kind[0] == "C":
            view = ref.at[pl.ds(where, count)]
        else:
            view = ref.at[pl.ds(pl.multiple_of(where + first, 16), count), :]
        i = INDEX[m]
        return pltpu.make_async_remote_copy(
            src_ref=view, dst_ref=view, send_sem=send.at[i], recv_sem=recv.at[i],
            device_id=target, device_id_type=MESH,
        )

    def sum_transfer(axis, k):
        ref, here = (x_sums, x) if axis == "x" else (y_sums, y)
        i = N_BULK + (k - 1 if axis == "x" else NX - 1 + k - 1)
        return pltpu.make_async_remote_copy(
            src_ref=ref.at[here], dst_ref=ref.at[here], send_sem=send.at[i], recv_sem=recv.at[i],
            device_id=near(axis, k), device_id_type=MESH,
        )

    query = lax.broadcasted_iota(jnp.int32, (QUERIES, BS), 0)
    spread = query == lax.broadcasted_iota(jnp.int32, (QUERIES, BS), 1)
    slot_of_lane = lax.broadcasted_iota(jnp.int32, (1, BS), 1) * (BS // 16)

    def look_up(ids, n, chunk_of, nothing, table, by_row):
        def one(s, carry):
            i, j = row_ids[s], col_ids[s]
            k = i - HALF + query
            k = jnp.where(k < 0, k + NB, jnp.where(k >= NB, k - NB, k))
            gap = jnp.abs(k - j)
            gap = jnp.minimum(gap, NB - gap)
            wanted = i * NB + k if by_row else k * NB + j
            wanted = jnp.where((query < PAIRS) & (gap <= HALF) & (i >= 0), wanted, -1)
            found = jnp.full((QUERIES, BS), -1, jnp.int32)
            for c in range(n):
                found = jnp.where(wanted == ids[c], slot_of_lane + chunk_of(c), found)
            found = jnp.max(found, axis=1, keepdims=True)
            found = jnp.where(found < 0, nothing, found)
            table[pl.ds(s, 1), :] = jnp.max(jnp.where(spread, found, 0), axis=0, keepdims=True)
            return carry

        lax.fori_loop(0, SLOTS, one, 0)

    def last(kinds):
        return max(i for i, (m, _, _) in enumerate(ORDER) if m[0] in kinds)

    def later(i, by):
        return next((n for n in range(i, len(ORDER)) if ORDER[n][2] >= ORDER[i][2] + by), len(ORDER) - 1)

    ids_left, ids_right, all_right = last(("CX", "CY")), last(("CS", "CZ")), last(("ZZ", "SS"))
    ids_known = max(ids_left, ids_right)
    looks = [
        pltpu.make_async_copy(left_at, left_look, local.at[0]),
        pltpu.make_async_copy(right_at, right_look, local.at[1]),
    ]
    x_known = later(all_right, 9.0)
    for m in FIRST:
        transfer(m).start()
    for i, (m, started, _) in enumerate(ORDER):
        transfer(m).wait_recv()
        for other in started:
            transfer(other).start()
        if i == ids_left:
            look_up(
                left_ids, N_LEFT, lambda c: (c % NX * NY + c // NX) * (LEFT_ROWS // 16), LEFT_ZERO // 16, left_at, True
            )
        if i == ids_right:
            look_up(right_ids, N_RIGHT, lambda c: c * (RIGHT_ROWS // 16), RIGHT_ZERO // 16, right_at, False)
        if i == later(ids_known, 2.0):
            for copy in looks:
                copy.start()
        if i == all_right:
            total = jnp.zeros((16, BS), jnp.float32)
            for c in range(N_RIGHT):
                total = total + right[pl.ds(c * RIGHT_ROWS + SUMS, 16), :].astype(jnp.float32)
            x_sums[x] = jnp.broadcast_to(jnp.sum(total, axis=0, keepdims=True), (8, BS))
        if i == later(all_right, 0.5):
            for k in range(1, NX):
                sum_transfer("x", k).start()
        if i == x_known:
            for k in range(1, NX):
                sum_transfer("x", k).wait_recv()
            total = x_sums[0]
            for k in range(1, NX):
                total = total + x_sums[k]
            y_sums[y] = total
        if i == later(x_known, 0.5):
            for k in range(1, NY):
                sum_transfer("y", k).start()
    for copy in looks:
        copy.wait()

    eye = lax.broadcasted_iota(jnp.int32, (BS, BS), 0) == lax.broadcasted_iota(jnp.int32, (BS, BS), 1)

    def one_slot(s, carry):
        def fetch(ref, table, q):
            return ref[pl.ds(table[s, q] * 16, BS), :]

        a = jnp.concatenate([fetch(left, left_look, q) for q in range(PAIRS + 1)], axis=1)
        b = jnp.concatenate([fetch(right, right_look, q) for q in range(PAIRS + 1)], axis=0)
        square = jnp.dot(a, b, preferred_element_type=jnp.float32)
        scale = jnp.where((row_ids[s] == col_ids[s]) & (row_ids[s] >= 0), 1.5, 0.0)
        factor[s] = (jnp.where(eye, scale, 0.0) - 0.5 * square).astype(jnp.bfloat16)
        return carry

    lax.fori_loop(0, SLOTS, one_slot, 0, unroll=4)

    for k in range(1, NY):
        sum_transfer("y", k).wait_recv()
    total = y_sums[0]
    for k in range(1, NY):
        total = total + y_sums[k]
    trace[0, 0] = jnp.max(total) * (1.0 / (NB * BS))

    for m in SIZE:
        transfer(m).wait_send()
    for axis, extent in (("x", NX), ("y", NY)):
        for k in range(1, extent):
            sum_transfer(axis, k).wait_send()


def shards(blocks, block_row, block_col):
    smem = pl.BlockSpec(memory_space=pltpu.SMEM)
    vmem = pl.BlockSpec(memory_space=pltpu.VMEM)
    factor, trace = pl.pallas_call(
        kernel,
        out_shape=(
            jax.ShapeDtypeStruct((SLOTS, BS, BS), jnp.bfloat16),
            jax.ShapeDtypeStruct((1, 1), jnp.float32),
        ),
        in_specs=[pl.BlockSpec(memory_space=pl.ANY), smem, smem],
        out_specs=(vmem, smem),
        scratch_shapes=[
            pltpu.VMEM((LEFT_ZERO + BS, BS), jnp.bfloat16),
            pltpu.VMEM((RIGHT_ZERO + BS, BS), jnp.bfloat16),
            pltpu.VMEM((N_LEFT, 1, BS), jnp.int32),
            pltpu.VMEM((N_RIGHT, 1, BS), jnp.int32),
            pltpu.VMEM((NX, 8, BS), jnp.float32),
            pltpu.VMEM((NY, 8, BS), jnp.float32),
            pltpu.VMEM((16, BS), jnp.int32),
            pltpu.VMEM((16, BS), jnp.int32),
            pltpu.SMEM((16, BS), jnp.int32),
            pltpu.SMEM((16, BS), jnp.int32),
            pltpu.SemaphoreType.DMA((N_SEM,)),
            pltpu.SemaphoreType.DMA((N_SEM,)),
            pltpu.SemaphoreType.DMA((2,)),
        ],
        compiler_params=pltpu.CompilerParams(collective_id=0, has_side_effects=True),
    )(blocks.reshape(BODY, BS), block_row.reshape(SLOTS), block_col.reshape(SLOTS))
    return factor[None, None], trace[0, 0]


def solution(mesh):
    torus = Mesh(mesh.devices.reshape(NZ, NCORE, NX, NY), AXES)
    return jax.shard_map(
        shards,
        mesh=torus,
        in_specs=(P(ROW, COL, None, None, None), P(ROW, COL, None), P(ROW, COL, None)),
        out_specs=(P(ROW, COL, None, None, None), P()),
        check_vma=False,
    )
```

```python
import functools
import heapq

import jax
import jax.numpy as jnp
from jax import lax
from jax.experimental import pallas as pl
from jax.experimental.pallas import tpu as pltpu
from jax.sharding import Mesh
from jax.sharding import PartitionSpec as P

HALF = 10
PAIRS = 2 * HALF + 1
QUERIES = 24
SLOTS = 12
BS = 128
NB = 384
AXES = ("z", "core", "x", "y")
NZ, NCORE, NX, NY = 12, 2, 4, 8
COL = ("x", "y")
ROW = ("z", "core")
MESH = pl.DeviceIdType.MESH

PART_A = (2, 3)
PART_B = (3, 4)
PART_Z = (6, 6)
BACKLOG = 4.0
Z_PATIENCE = 1.0
BODY = SLOTS * BS
LEFT_ROWS = BODY
SUMS = BODY
RIGHT_ROWS = BODY + 16
NOTHING = NB * NB
N_LEFT, N_RIGHT = NX * NY, NZ * NCORE
LEFT_ZERO = N_LEFT * LEFT_ROWS
RIGHT_ZERO = N_RIGHT * RIGHT_ROWS


def plan():
    size, need, rows = {}, {}, {}

    def add(name, link, span, after):
        size[name] = (link, (span[1] - span[0]) / BS)
        need[name] = after
        rows[name] = (span[0], span[1] - span[0])

    def spans(parts, first):
        for count in parts:
            yield (first * BS, (first + count) * BS)
            first += count

    for p, span in enumerate(spans(PART_A, 0)):
        for d in "RL":
            add(("AX", d, 1, 0, p), "x" + d, span, [])
        d = "RL"[p % 2]
        add(("AX", d, 2, 0, p), "x" + d, span, [("AX", d, 1, 0, p)])
        came = {0: [], -1: [("AX", "R", 1, 0, p)], 1: [("AX", "L", 1, 0, p)], 2: [("AX", d, 2, 0, p)]}
        for dx in (0, -1, 1, 2):
            for d in "UD":
                add(("AY", d, 1, dx, p), "y" + d, span, came[dx])
                for h in (2, 3):
                    add(("AY", d, h, dx, p), "y" + d, span, [("AY", d, h - 1, dx, p)])
            d = "U" if (dx in (0, -1)) == (p % 2 == 0) else "D"
            add(("AY", d, 4, dx, p), "y" + d, span, [("AY", d, 3, dx, p)])
    for p, span in enumerate(spans(PART_B, sum(PART_A))):
        for d in "UD":
            add(("BY", d, 1, 0, p), "y" + d, span, [])
            for h in (2, 3):
                add(("BY", d, h, 0, p), "y" + d, span, [("BY", d, h - 1, 0, p)])
        d = "UD"[p % 2]
        add(("BY", d, 4, 0, p), "y" + d, span, [("BY", d, 3, 0, p)])
        came = {0: [], 4: [("BY", d, 4, 0, p)]}
        for h in (1, 2, 3):
            came[-h], came[h] = [("BY", "U", h, 0, p)], [("BY", "D", h, 0, p)]
        for dy in (0, -1, 1, -2, 2, -3, 3, 4):
            for d in "RL":
                add(("BX", d, 1, dy, p), "x" + d, span, came[dy])
            d = "R" if (dy in (0, -1, 2, -3)) == (p % 2 == 0) else "L"
            add(("BX", d, 2, dy, p), "x" + d, span, [("BX", d, 1, dy, p)])
    for p, span in enumerate(spans(PART_Z, 0)):
        if p == len(PART_Z) - 1:
            span = (span[0], RIGHT_ROWS)
        add(("SS", "O", 0, 0, p), "s", span, [])
        for d in "UD":
            for h in range(1, 7 if d == "UD"[p % 2] else 6):
                add(("ZZ", d, h, 0, p), "z" + d, span, [("ZZ", d, h - 1, 0, p)] if h > 1 else [])
                add(("SS", d, h, 0, p), "s", span, [("ZZ", d, h, 0, p)])
    add(("CX", "R", 1), "xR", (0, 1), [])
    add(("CX", "L", 1), "xL", (0, 1), [])
    add(("CX", "R", 2), "xR", (0, 1), [("CX", "R", 1)])
    for d in "UD":
        for h in range(1, 5 if d == "U" else 4):
            after = [("CY", d, h - 1)] if h > 1 else [("CX", "R", 1), ("CX", "L", 1), ("CX", "R", 2)]
            add(("CY", d, h), "y" + d, (0, NX), after)
    add(("CS", "O", 0), "s", (0, 1), [])
    for d in "UD":
        for h in range(1, 7 if d == "U" else 6):
            add(("CZ", d, h), "z" + d, (0, NCORE), [("CZ", d, h - 1)] if h > 1 else [("CS", "O", 0)])
    return size, need, rows


def expected(size, need):
    after = {m: [] for m in size}
    for m, waits in need.items():
        for other in waits:
            after[other].append(m)
    length = {}

    def duration(m):
        link, blocks = size[m]
        return blocks * (0.05 if link == "s" else 0.706)

    def chain(m):
        if m not in length:
            length[m] = 1.6 + duration(m) + max([chain(n) for n in after[m]], default=0.0)
        return length[m]

    number = {m: i for i, m in enumerate(size)}
    rank = {m: (m[0][0] != "C", -chain(m), number[m]) for m in size}
    pending = {m: set(waits) for m, waits in need.items()}
    free, queue, waiting = {}, [], {}

    def start(now):
        started = []
        for link in sorted(waiting):
            ready = sorted(waiting[link], key=lambda m: rank[m])
            while ready and (link == "s" or free.get(link, 0.0) - now < BACKLOG):
                m = ready.pop(0)
                free[link] = max(now, free.get(link, 0.0)) + duration(m)
                wait = 1.6 + Z_PATIENCE * (link[0] == "z")
                heapq.heappush(queue, (round(free[link] + wait, 6), len(started), number[m], m))
                started.append(m)
            waiting[link] = ready
        return started

    def release(m):
        waiting.setdefault(size[m][0], []).append(m)

    for m in size:
        if not need[m]:
            release(m)
    first, order, now = start(0.0), [], 0.0
    while queue:
        when, _, _, m = heapq.heappop(queue)
        now = max(now, when) + 0.05
        for other in after[m]:
            pending[other].discard(m)
            if not pending[other]:
                release(other)
        order.append((m, start(now), now))
    return first, order


SIZE, NEED, ROWS = plan()
FIRST, ORDER = expected(SIZE, NEED)
INDEX = {m: i for i, m in enumerate(SIZE)}
N_BULK = len(SIZE)
N_SEM = N_BULK + NX - 1 + NY - 1


def kernel(
    blocks, row_ids, col_ids, factor, trace, left, right, left_ids, right_ids, x_sums, y_sums, left_at, right_at,
    left_look, right_look, send, recv, local,
):
    z, core, x, y = (lax.axis_index(a) for a in AXES)

    def at(base, shift, extent):
        return lax.rem(base + (shift + extent), extent)

    def left_chunk(dx, dy):
        return (at(x, dx, NX) * NY + at(y, dy, NY)) * LEFT_ROWS

    def right_chunk(dz, which):
        return (at(z, dz, NZ) * NCORE + which) * RIGHT_ROWS

    def near(axis, shift):
        base, extent = {"x": (x, NX), "y": (y, NY), "z": (z, NZ)}[axis]
        return {axis: at(base, shift, extent)}

    own_left = left_chunk(0, 0)
    own_right = right_chunk(0, core)
    mine = [
        pltpu.make_async_copy(
            blocks, left.at[pl.ds(pl.multiple_of(own_left, 16), BODY), :], local.at[0]
        ),
        pltpu.make_async_copy(
            blocks, right.at[pl.ds(pl.multiple_of(own_right, 16), BODY), :], local.at[1]
        ),
    ]
    for copy in mine:
        copy.start()

    barrier = pltpu.get_barrier_semaphore()
    partners = [near(a, s) for a in ("x", "y", "z") for s in (1, -1)] + [{"core": 1 - core}]
    for partner in partners:
        pl.semaphore_signal(barrier, inc=1, device_id=partner, device_id_type=MESH)

    lane = lax.broadcasted_iota(jnp.int32, (1, BS), 1)
    code = jnp.full((1, BS), NOTHING, jnp.int32)
    for t in range(SLOTS):
        value = jnp.where(row_ids[t] >= 0, row_ids[t] * NB + col_ids[t], NOTHING)
        code = jnp.where(lane == t, value, code)
    left_ids[y * NX + x] = code
    right_ids[z * NCORE + core] = code
    left[pl.ds(LEFT_ZERO, BS), :] = jnp.zeros((BS, BS), jnp.bfloat16)
    right[pl.ds(RIGHT_ZERO, BS), :] = jnp.zeros((BS, BS), jnp.bfloat16)

    for copy in mine:
        copy.wait()

    total = jnp.zeros((8, BS), jnp.float32)
    for t in range(SLOTS):
        block = left[pl.ds(pl.multiple_of(own_left + t * BS, 16), BS), :].astype(jnp.float32)
        folded = jnp.sum((block * block).reshape(BS // 8, 8, BS), axis=0)
        total = total + jnp.where(row_ids[t] >= 0, folded, 0.0)
    part = jnp.sum(jnp.sum(total, axis=1, keepdims=True), axis=0, keepdims=True)
    high = part.astype(jnp.bfloat16).astype(jnp.float32)
    middle = (part - high).astype(jnp.bfloat16).astype(jnp.float32)
    low = part - high - middle
    row_iota = lax.broadcasted_iota(jnp.int32, (16, BS), 0)
    piece = jnp.where(row_iota == 0, high, jnp.where(row_iota == 1, middle, low))
    right[pl.ds(pl.multiple_of(own_right + SUMS, 16), 16), :] = jnp.where(
        row_iota < 3, piece, 0.0
    ).astype(jnp.bfloat16)

    pl.semaphore_wait(barrier, len(partners))

    def transfer(m):
        kind, d, h = m[:3]
        first, count = ROWS[m]
        sign = -1 if d in "RU" else 1
        step = sign * (h - 1)
        if kind in ("CX", "CY"):
            ref = left_ids
            where = y * NX + at(x, step, NX) if kind == "CX" else at(y, step, NY) * NX
            target = near(kind[1].lower(), -sign)
        elif kind in ("CS", "CZ"):
            ref = right_ids
            where = z * NCORE + core if kind == "CS" else at(z, step, NZ) * NCORE
            target = {"core": 1 - core} if kind == "CS" else near("z", -sign)
        elif kind in ("ZZ", "SS"):
            if kind == "SS":
                where = right_chunk(sign * h if h else 0, core)
                target = {"core": 1 - core}
            else:
                where = right_chunk(step, core)
                target = near("z", -sign)
            ref = right
        else:
            if kind == "AX":
                where = left_chunk(step, 0)
            elif kind == "BX":
                where = left_chunk(step, m[3])
            elif kind == "BY":
                where = left_chunk(0, step)
            else:
                where = left_chunk(m[3], step)
            target = near("x" if kind in ("AX", "BX") else "y", -sign)
            ref = left
        if kind[0] == "C":
            view = ref.at[pl.ds(where, count)]
        else:
            view = ref.at[pl.ds(pl.multiple_of(where + first, 16), count), :]
        i = INDEX[m]
        return pltpu.make_async_remote_copy(
            src_ref=view, dst_ref=view, send_sem=send.at[i], recv_sem=recv.at[i],
            device_id=target, device_id_type=MESH,
        )

    def sum_transfer(axis, k):
        ref, here = (x_sums, x) if axis == "x" else (y_sums, y)
        i = N_BULK + (k - 1 if axis == "x" else NX - 1 + k - 1)
        return pltpu.make_async_remote_copy(
            src_ref=ref.at[here], dst_ref=ref.at[here], send_sem=send.at[i], recv_sem=recv.at[i],
            device_id=near(axis, k), device_id_type=MESH,
        )

    query = lax.broadcasted_iota(jnp.int32, (QUERIES, BS), 0)
    spread = query == lax.broadcasted_iota(jnp.int32, (QUERIES, BS), 1)
    slot_of_lane = lax.broadcasted_iota(jnp.int32, (1, BS), 1) * (BS // 16)

    def look_up(ids, n, chunk_of, nothing, table, by_row):
        def one(s, carry):
            i, j = row_ids[s], col_ids[s]
            k = i - HALF + query
            k = jnp.where(k < 0, k + NB, jnp.where(k >= NB, k - NB, k))
            gap = jnp.abs(k - j)
            gap = jnp.minimum(gap, NB - gap)
            wanted = i * NB + k if by_row else k * NB + j
            wanted = jnp.where((query < PAIRS) & (gap <= HALF) & (i >= 0), wanted, -1)
            found = jnp.full((QUERIES, BS), -1, jnp.int32)
            for c in range(n):
                found = jnp.where(wanted == ids[c], slot_of_lane + chunk_of(c), found)
            found = jnp.max(found, axis=1, keepdims=True)
            found = jnp.where(found < 0, nothing, found)
            table[pl.ds(s, 1), :] = jnp.max(jnp.where(spread, found, 0), axis=0, keepdims=True)
            return carry

        lax.fori_loop(0, SLOTS, one, 0)

    def last(kinds):
        return max(i for i, (m, _, _) in enumerate(ORDER) if m[0] in kinds)

    def later(i, by):
        return next((n for n in range(i, len(ORDER)) if ORDER[n][2] >= ORDER[i][2] + by), len(ORDER) - 1)

    ids_left, ids_right, all_right = last(("CX", "CY")), last(("CS", "CZ")), last(("ZZ", "SS"))
    ids_known = max(ids_left, ids_right)
    looks = [
        pltpu.make_async_copy(left_at, left_look, local.at[0]),
        pltpu.make_async_copy(right_at, right_look, local.at[1]),
    ]
    x_known = later(all_right, 9.0)
    leaving = [(m, 0.0) for m in FIRST]
    for m in FIRST:
        transfer(m).start()
    for i, (m, started, now) in enumerate(ORDER):
        transfer(m).wait_recv()
        leaving += [(other, now) for other in started]
        while leaving and now - leaving[0][1] > 20.0:
            transfer(leaving.pop(0)[0]).wait_send()
        for other in started:
            transfer(other).start()
        if i == ids_left:
            look_up(
                left_ids, N_LEFT, lambda c: (c % NX * NY + c // NX) * (LEFT_ROWS // 16), LEFT_ZERO // 16, left_at, True
            )
        if i == ids_right:
            look_up(right_ids, N_RIGHT, lambda c: c * (RIGHT_ROWS // 16), RIGHT_ZERO // 16, right_at, False)
        if i == later(ids_known, 2.0):
            for copy in looks:
                copy.start()
        if i == all_right:
            total = jnp.zeros((16, BS), jnp.float32)
            for c in range(N_RIGHT):
                total = total + right[pl.ds(c * RIGHT_ROWS + SUMS, 16), :].astype(jnp.float32)
            x_sums[x] = jnp.broadcast_to(jnp.sum(total, axis=0, keepdims=True), (8, BS))
        if i == later(all_right, 0.5):
            for k in range(1, NX):
                sum_transfer("x", k).start()
        if i == x_known:
            for k in range(1, NX):
                sum_transfer("x", k).wait_recv()
            total = x_sums[0]
            for k in range(1, NX):
                total = total + x_sums[k]
            y_sums[y] = total
        if i == later(x_known, 0.5):
            for k in range(1, NY):
                sum_transfer("y", k).start()
    for copy in looks:
        copy.wait()

    eye = lax.broadcasted_iota(jnp.int32, (BS, BS), 0) == lax.broadcasted_iota(jnp.int32, (BS, BS), 1)

    def one_slot(s, carry):
        def fetch(ref, table, q):
            return ref[pl.ds(table[s, q] * 16, BS), :]

        a = jnp.concatenate([fetch(left, left_look, q) for q in range(PAIRS + 1)], axis=1)
        b = jnp.concatenate([fetch(right, right_look, q) for q in range(PAIRS + 1)], axis=0)
        square = jnp.dot(a, b, preferred_element_type=jnp.float32)
        scale = jnp.where((row_ids[s] == col_ids[s]) & (row_ids[s] >= 0), 1.5, 0.0)
        factor[s] = (jnp.where(eye, scale, 0.0) - 0.5 * square).astype(jnp.bfloat16)
        return carry

    lax.fori_loop(0, SLOTS, one_slot, 0, unroll=6)

    for k in range(1, NY):
        sum_transfer("y", k).wait_recv()
    total = y_sums[0]
    for k in range(1, NY):
        total = total + y_sums[k]
    trace[0, 0] = jnp.max(total) * (1.0 / (NB * BS))

    for m, _ in leaving:
        transfer(m).wait_send()
    for axis, extent in (("x", NX), ("y", NY)):
        for k in range(1, extent):
            sum_transfer(axis, k).wait_send()


def shards(blocks, block_row, block_col):
    smem = pl.BlockSpec(memory_space=pltpu.SMEM)
    vmem = pl.BlockSpec(memory_space=pltpu.VMEM)
    factor, trace = pl.pallas_call(
        kernel,
        out_shape=(
            jax.ShapeDtypeStruct((SLOTS, BS, BS), jnp.bfloat16),
            jax.ShapeDtypeStruct((1, 1), jnp.float32),
        ),
        in_specs=[pl.BlockSpec(memory_space=pl.ANY), smem, smem],
        out_specs=(vmem, smem),
        scratch_shapes=[
            pltpu.VMEM((LEFT_ZERO + BS, BS), jnp.bfloat16),
            pltpu.VMEM((RIGHT_ZERO + BS, BS), jnp.bfloat16),
            pltpu.VMEM((N_LEFT, 1, BS), jnp.int32),
            pltpu.VMEM((N_RIGHT, 1, BS), jnp.int32),
            pltpu.VMEM((NX, 8, BS), jnp.float32),
            pltpu.VMEM((NY, 8, BS), jnp.float32),
            pltpu.VMEM((16, BS), jnp.int32),
            pltpu.VMEM((16, BS), jnp.int32),
            pltpu.SMEM((16, BS), jnp.int32),
            pltpu.SMEM((16, BS), jnp.int32),
            pltpu.SemaphoreType.DMA((N_SEM,)),
            pltpu.SemaphoreType.DMA((N_SEM,)),
            pltpu.SemaphoreType.DMA((2,)),
        ],
        compiler_params=pltpu.CompilerParams(collective_id=0, has_side_effects=True),
    )(blocks.reshape(BODY, BS), block_row.reshape(SLOTS), block_col.reshape(SLOTS))
    return factor[None, None], trace[0, 0]


def solution(mesh):
    torus = Mesh(mesh.devices.reshape(NZ, NCORE, NX, NY), AXES)
    return jax.shard_map(
        shards,
        mesh=torus,
        in_specs=(P(ROW, COL, None, None, None), P(ROW, COL, None), P(ROW, COL, None)),
        out_specs=(P(ROW, COL, None, None, None), P()),
        check_vma=False,
    )
```
